32 devices in a mesh: segment: 2 (over core), expert: 4 (over z), tensor: 4 (over y, x).
Axes of the slice: x: 2, y: 2, z: 4, core: 2. Of those that a mesh axis runs over, the one named last changes fastest.
Arguments:
- activations: bfloat16 [2, 256, 2560], P('segment', 'expert', 'tensor'), may hold values from -48 to 48
- expert_ids: int32 [2, 256, 6], P(None, 'expert'), may hold values from 0 to 7, as said below
- route_weights: float32 [2, 256, 6], P(None, 'expert'), may hold values from 0.05 to 1
- gain_dense: float32 [2560], replicated, may hold values from 0.25 to 1.75
- gain_expert: float32 [2560], replicated, may hold values from 0.25 to 1.75
- dense_gate: bfloat16 [2560, 6144], P('expert', 'tensor'), may hold values from -0.125 to 0.125
- dense_up: bfloat16 [2560, 6144], P('expert', 'tensor'), may hold values from -0.125 to 0.125
- dense_down: bfloat16 [2560, 6144], P('expert', 'tensor'), may hold values from -0.078125 to 0.078125
- expert_gate: bfloat16 [8, 2560, 1536], P('expert', None, 'tensor'), may hold values from -0.125 to 0.125
- expert_up: bfloat16 [8, 2560, 1536], P('expert', None, 'tensor'), may hold values from -0.125 to 0.125
- expert_down: bfloat16 [8, 1536, 2560], P('expert', 'tensor'), may hold values from -0.15625 to 0.15625
Outputs:
- sections: bfloat16 [2, 2, 256, 2560], P('segment', None, 'expert', 'tensor')
The draws below stay inside these ranges and needn't reach their ends.
Inputs may be any that keep to these rules, and one draw needn't show every extreme that they name: `expert_ids`: each token names 6 different experts. Split each micro-batch's tokens into blocks of 64 in order: no expert is named by more than 64 tokens of one block, and in every micro-batch one expert is named by exactly 64 tokens of every block.
All inputs are finite; a program needn't handle non-finite values.
Results may differ from the reference program's by a relative error of at most 0.009.
Values may be sent and summed in bfloat16 or wider, within the bound.
No kernel may reach another device: no remote copies, remote signals or barrier semaphores. Data moves between devices by JAX's collectives and lax.ppermute only.
A program may use at most 128 MiB of HBM per device.

```python
import math
import jax
import jax.numpy as jnp
from jax import lax

D = 2560
FF = 6144
H = 1536
TOP = 6
MICRO = 2
TOK_DEV = 64
EXPERTS = 8
TOKENS = 256
CAP = 64
N_EXPERT = 4
N_TENSOR = 4


def draw_activations(key, part):
    key_cols, key_rows, key_values = jax.random.split(jax.random.fold_in(key, 11), 3)
    position = jnp.arange(D, dtype=jnp.float32) / D
    row_scale = jnp.exp(jax.random.uniform(key_rows, (MICRO, TOKENS, 1), jnp.float32, -0.8, 0.8))
    trend = 2.3 * (position - 0.5)
    column_scale = jnp.exp(trend + jax.random.uniform(key_cols, (D,), jnp.float32, -0.4, 0.4))
    values = jax.random.truncated_normal(key_values, -4.0, 4.0, (MICRO, TOKENS, D), jnp.float32)
    return (values * column_scale * row_scale).astype(jnp.bfloat16)


def draw_expert_ids(key, part):
    blocks = TOKENS // TOK_DEV
    hot_experts = jax.random.randint(jax.random.fold_in(key, 21), (MICRO,), 0, EXPERTS)
    block_keys = jax.random.split(jax.random.fold_in(key, 22), MICRO * blocks)
    block_keys = block_keys.reshape((MICRO, blocks) + block_keys.shape[1:])

    def one_block(block_key, hot_expert):
        key_pick, key_order, key_within = jax.random.split(block_key, 3)
        others = jnp.arange(EXPERTS - 1, dtype=jnp.int32)
        others = others + (others >= hot_expert).astype(jnp.int32)
        tickets = jnp.repeat(others, CAP)
        chosen = tickets[jax.random.permutation(key_pick, tickets.shape[0])[:TOK_DEV * TOP - CAP]]
        labels = jnp.sort(jnp.concatenate([jnp.full((CAP,), hot_expert, jnp.int32), chosen]))
        dealt_rows = labels.reshape(TOP, TOK_DEV).T
        dealt_rows = dealt_rows[jax.random.permutation(key_order, TOK_DEV)]
        orders = jax.vmap(lambda row_key: jax.random.permutation(row_key, TOP))(jax.random.split(key_within, TOK_DEV))
        return jnp.take_along_axis(dealt_rows, orders, axis=1)
    drawn_ids = jax.vmap(jax.vmap(one_block, in_axes=(0, None)), in_axes=(0, 0))(block_keys, hot_experts)
    return drawn_ids.reshape(MICRO, TOKENS, TOP).astype(jnp.int32)


def block_scale(key, extent, cuts, smallest, largest):
    def one(axis_at, blocks):
        heights = jax.random.uniform(jax.random.fold_in(jax.random.fold_in(key, 6), axis_at), (blocks,), jnp.float32, smallest / len(cuts), largest / len(cuts))
        return jnp.repeat(jnp.exp(heights), extent[axis_at] // blocks).reshape((-1,) + (1,) * (len(extent) - axis_at - 1))

    gain = one(*cuts[0])
    for cut in cuts[1:]:
        gain = gain * one(*cut)
    return gain


def noise(stream_key, extent, deviation, reach, cuts=(), kind=jnp.bfloat16):
    drawn = jax.random.normal(stream_key, extent, jnp.float32) * deviation
    if len(cuts) > 0:
        drawn = block_scale(stream_key, extent, cuts, -0.22, 0.18) * drawn
    return jnp.clip(drawn, min=-reach, max=reach).astype(kind)


def setup_inputs(seed: int = 0) -> dict:
    arg_keys = jax.random.split(jax.random.key(seed), 12)
    return {
        "activations": draw_activations(jax.random.fold_in(arg_keys[11], 71), 0),
        "expert_ids": draw_expert_ids(jax.random.fold_in(arg_keys[11], 71), 0),
        "route_weights": jnp.clip(jnp.exp(math.log(1.0) - 2.9957323 * jax.random.uniform(arg_keys[2], (MICRO, TOKENS, TOP), jnp.float32) ** block_scale(arg_keys[2], (MICRO, TOKENS, TOP), ((1, 4),), -0.2, 0.2)), 0.05, 1.0),
        "gain_dense": jnp.clip(1.0 + 0.15 * jax.random.normal(arg_keys[3], (D,), jnp.float32), 0.25, 1.75),
        "gain_expert": jnp.clip(1.0 + 0.15 * jax.random.normal(arg_keys[4], (D,), jnp.float32), 0.25, 1.75),
        "dense_gate": noise(arg_keys[5], (D, FF), D ** -0.5, 0.125, ((0, 4), (1, 4))),
        "dense_up": noise(arg_keys[6], (D, FF), D ** -0.5, 0.125, ((0, 4), (1, 4))),
        "dense_down": noise(arg_keys[7], (D, FF), FF ** -0.5, 0.078125, ((0, 4), (1, 4))),
        "expert_gate": noise(arg_keys[8], (EXPERTS, D, H), D ** -0.5, 0.125, ((0, 4), (2, 4))),
        "expert_up": noise(arg_keys[9], (EXPERTS, D, H), D ** -0.5, 0.125, ((0, 4), (2, 4))),
        "expert_down": noise(arg_keys[10], (EXPERTS, H, D), H ** -0.5, 0.15625, ((0, 4), (1, 4))),
    }


EPSILON = 1e-06

def normalize(values, gain_row):
    inverse = lax.rsqrt(lax.optimization_barrier(jnp.mean(values * values, axis=-1, keepdims=True)) + EPSILON)
    return values * inverse * gain_row

def mixture(normed, expert_ids_block, route_block, expert_gate, expert_up, expert_down):
    flat_ids = expert_ids_block.reshape(-1)
    picks_total = flat_ids.shape[0]
    blocks = jnp.arange(picks_total, dtype=jnp.int32) // (TOK_DEV * TOP)
    one_hot = (flat_ids[:, None] == jnp.arange(EXPERTS, dtype=jnp.int32)[None, :]).astype(jnp.int32)
    running = jnp.cumsum(one_hot.reshape(N_EXPERT, TOK_DEV * TOP, EXPERTS), axis=1).reshape(picks_total, EXPERTS)
    ranks = lax.optimization_barrier(jnp.sum((running - 1) * one_hot, axis=1))
    slots = ((flat_ids * N_EXPERT + blocks) * CAP + ranks).astype(jnp.int32)
    owners = jnp.arange(picks_total, dtype=jnp.int32) // TOP
    rows_per_expert = N_EXPERT * CAP
    sources = jnp.full((EXPERTS * rows_per_expert,), TOKENS, jnp.int32).at[slots].set(owners)
    shares = jnp.zeros((EXPERTS * rows_per_expert,), jnp.float32).at[slots].set(route_block.reshape(-1))
    padded = jnp.concatenate([normed, jnp.zeros((1, D), normed.dtype)], axis=0)
    hidden_part = H // N_TENSOR

    def one_expert(totals, inputs):
        gate_weight, up_weight, down_weight, source_rows, share_rows = inputs
        values = padded[source_rows]
        gate_sums = jnp.dot(values, gate_weight, preferred_element_type=jnp.float32)
        upward = jnp.dot(values, up_weight, preferred_element_type=jnp.float32)
        hidden = (jax.nn.silu(gate_sums) * upward).astype(jnp.bfloat16)
        output = jnp.zeros((rows_per_expert, D), jnp.float32)
        for block_index in range(N_TENSOR):
            first_unit = block_index * hidden_part
            piece_sum = jnp.dot(hidden[:, first_unit:first_unit + hidden_part], down_weight[first_unit:first_unit + hidden_part], preferred_element_type=jnp.float32).astype(jnp.bfloat16)
            output = output + lax.optimization_barrier(piece_sum).astype(jnp.float32)
        rounded = lax.optimization_barrier(output.astype(jnp.bfloat16)).astype(jnp.float32)
        totals = totals.at[source_rows].add(share_rows[:, None] * rounded)
        return (totals, None)
    totals, unused = lax.scan(one_expert, jnp.zeros((TOKENS + 1, D), jnp.float32), (expert_gate, expert_up, expert_down, sources.reshape(EXPERTS, rows_per_expert), shares.reshape(EXPERTS, rows_per_expert)))
    return totals[:TOKENS]

def reference(activations, expert_ids, route_weights, gain_dense, gain_expert, dense_gate, dense_up, dense_down, expert_gate, expert_up, expert_down):
    firsts = []
    seconds = []
    for micro_index in range(MICRO):
        inputs = activations[micro_index].astype(jnp.float32)
        normed = normalize(inputs, gain_dense).astype(jnp.bfloat16)
        gate_sums = jnp.dot(normed, dense_gate, preferred_element_type=jnp.float32)
        upward = jnp.dot(normed, dense_up, preferred_element_type=jnp.float32)
        hidden = (jax.nn.silu(gate_sums) * upward).astype(jnp.bfloat16)
        projected = lax.dot_general(hidden, dense_down, (((1,), (1,)), ((), ())), preferred_element_type=jnp.float32)
        middle = (inputs + projected).astype(jnp.bfloat16)
        middle_wide = middle.astype(jnp.float32)
        expert_in = normalize(middle_wide, gain_expert).astype(jnp.bfloat16)
        mixed = mixture(expert_in, expert_ids[micro_index], route_weights[micro_index], expert_gate, expert_up, expert_down)
        firsts.append(middle)
        seconds.append((middle_wide + mixed).astype(jnp.bfloat16))
    return jnp.stack([jnp.stack(firsts), jnp.stack(seconds)])
```

```python
import jax
import jax.numpy as jnp
from jax import lax
from jax.sharding import PartitionSpec as P

EPSILON = 1e-06


def shifted(block, axis, distance):
    devices = range(lax.axis_size(axis))
    route = [((i - distance) % len(devices), i) for i in devices]
    return lax.ppermute(block, axis, route)


def normalize(values, gain_row):
    inverse = lax.rsqrt(jnp.mean(values * values, axis=-1, keepdims=True) + EPSILON)
    return values * inverse * gain_row


def dense_prepare(micro_block, gain_dense):
    micro_count, tokens_here, quarter = micro_block.shape
    whole_rows = lax.all_gather(micro_block, "tensor", axis=2, tiled=True)
    full_width = whole_rows.shape[2]
    normed = normalize(whole_rows.astype(jnp.float32), gain_dense).astype(jnp.bfloat16)
    return normed.reshape(micro_count * tokens_here, full_width)


def dense_finish(micro_block, partial_value):
    micro_count, tokens_here, quarter = micro_block.shape
    summed = lax.psum_scatter(
        partial_value.reshape(micro_count, tokens_here, partial_value.shape[1]).astype(
            jnp.bfloat16
        ),
        "tensor",
        scatter_dimension=2,
        tiled=True,
    ).astype(jnp.float32)
    return (micro_block.astype(jnp.float32) + summed).astype(jnp.bfloat16)


def dense_folded(activations, gain_dense, dense_gate, dense_up, dense_down):
    normed = dense_prepare(activations, gain_dense)
    gate_sums = jnp.dot(
        normed,
        lax.all_gather(dense_gate, "expert", axis=0, tiled=True),
        preferred_element_type=jnp.float32,
    )
    upward = jnp.dot(
        normed,
        lax.all_gather(dense_up, "expert", axis=0, tiled=True),
        preferred_element_type=jnp.float32,
    )
    hidden = (jax.nn.silu(gate_sums) * upward).astype(jnp.bfloat16)
    partial_value = lax.dot_general(
        hidden,
        lax.all_gather(dense_down, "expert", axis=0, tiled=True),
        (((1,), (1,)), ((), ())),
        preferred_element_type=jnp.float32,
    )
    return dense_finish(activations, partial_value)


def route_slots(expert_ids_block, local_count, groups, capacity):
    tokens_here, picks = expert_ids_block.shape
    flat_ids = expert_ids_block.reshape(-1)
    experts_all = local_count * groups
    one_hot = (flat_ids[:, None] == jnp.arange(experts_all, dtype=jnp.int32)[None, :]).astype(
        jnp.int32
    )
    ranks = jnp.sum((jnp.cumsum(one_hot, axis=0) - 1) * one_hot, axis=1)
    slots = (flat_ids % local_count * groups + flat_ids // local_count) * capacity + ranks
    owners = jnp.arange(tokens_here * picks, dtype=jnp.int32) // picks
    sources = jnp.full((experts_all * capacity,), tokens_here, jnp.int32).at[slots].set(owners)
    return (slots, sources)


def place_rows(normed, sources, local_count, groups, capacity):
    padded = jnp.concatenate([normed, jnp.zeros((1, normed.shape[1]), normed.dtype)], axis=0)
    return padded[sources].reshape(local_count, groups, capacity, normed.shape[1])


def expert_block(
    middle, expert_ids_block, route_block, gain_expert, expert_gate, expert_up, expert_down
):
    tokens_here, quarter = middle.shape
    picks = expert_ids_block.shape[1]
    groups = lax.axis_size("expert")
    local_count, full_width, hidden_part = expert_gate.shape
    capacity = min(tokens_here, 2 * (tokens_here * picks // (local_count * groups)))
    slots, sources = route_slots(expert_ids_block, local_count, groups, capacity)
    middle_wide = middle.astype(jnp.float32)
    received_rows = groups * capacity
    tensor_index = lax.axis_index("tensor")
    square_sums = lax.psum(jnp.sum(middle_wide * middle_wide, axis=1), "tensor")
    inverse = lax.rsqrt(square_sums / full_width + EPSILON)
    gain_part = lax.dynamic_slice_in_dim(gain_expert, tensor_index * quarter, quarter, 0)
    normed = (middle_wide * inverse[:, None] * gain_part).astype(jnp.bfloat16)
    outgoing = place_rows(normed, sources, local_count, groups, capacity)
    arrived = lax.all_to_all(outgoing, "expert", split_axis=1, concat_axis=1, tiled=True)
    arrived = arrived.reshape(local_count, received_rows, quarter)
    slice_part = lax.all_gather(arrived, "tensor", axis=2, tiled=True)
    gate_sums = jnp.einsum(
        "lrc,lch->lrh", slice_part, expert_gate, preferred_element_type=jnp.float32
    )
    upward = jnp.einsum("lrc,lch->lrh", slice_part, expert_up, preferred_element_type=jnp.float32)
    hidden = (jax.nn.silu(gate_sums) * upward).astype(jnp.bfloat16)
    partial_value = jnp.einsum(
        "lrh,lhd->lrd", hidden, expert_down, preferred_element_type=jnp.float32
    )
    summed = lax.psum_scatter(
        partial_value.astype(jnp.bfloat16), "tensor", scatter_dimension=2, tiled=True
    )
    returned = lax.all_to_all(
        summed.reshape(local_count, groups, capacity, quarter),
        "expert",
        split_axis=1,
        concat_axis=1,
        tiled=True,
    )
    picked = returned.reshape(local_count * groups * capacity, quarter)[slots]
    picked = picked.reshape(tokens_here, picks, quarter).astype(jnp.float32)
    mixed = jnp.sum(route_block[:, :, None] * picked, axis=1)
    return (middle_wide + mixed).astype(jnp.bfloat16)


def general_body(
    activations,
    expert_ids,
    route_weights,
    gain_dense,
    gain_expert,
    dense_gate,
    dense_up,
    dense_down,
    expert_gate,
    expert_up,
    expert_down,
):
    segment_index = lax.axis_index("segment")
    own_middle = dense_folded(activations, gain_dense, dense_gate, dense_up, dense_down)
    other_middle = shifted(own_middle, "segment", 1)
    middles = jnp.where(
        segment_index == 0,
        jnp.concatenate([own_middle, other_middle], axis=0),
        jnp.concatenate([other_middle, own_middle], axis=0),
    )
    finals = jnp.stack(
        [
            expert_block(
                middles[position],
                expert_ids[position],
                route_weights[position],
                gain_expert,
                expert_gate,
                expert_up,
                expert_down,
            )
            for position in range(middles.shape[0])
        ]
    )
    sections = jnp.where(segment_index == 0, middles, finals)
    return sections[None]


def swap(block, axis, distance):
    devices = range(lax.axis_size(axis))
    return lax.ppermute(block, axis, [(i, i ^ distance) for i in devices])


def transposed(block):
    size = lax.axis_size("tensor")
    route = [(a * size + b, b * size + a) for a in range(size) for b in range(size)]
    return lax.ppermute(block, ("expert", "tensor"), route)


def gathered(block, axis):
    size = lax.axis_size(axis)
    arrived = {d: swap(block, axis, d) for d in range(size - 1, 0, -1)}
    return [block] + [arrived[d] for d in range(1, size)]


def traded(blocks, axis):
    size = lax.axis_size(axis)
    sent = {d: swap(blocks[d].astype(jnp.bfloat16), axis, d) for d in range(size - 1, 0, -1)}
    total = blocks[0].astype(jnp.float32)
    for d in range(1, size):
        total = total + sent[d].astype(jnp.float32)
    return total


def pick(stacked, index):
    return lax.dynamic_index_in_dim(stacked, index, 0, keepdims=False)


def two_parts(values):
    high = lax.reduce_precision(values, 8, 7)
    return jnp.concatenate([high, values - high], axis=1).astype(jnp.bfloat16)


def padded_columns(values):
    extra = -values.shape[1] % 128
    return jnp.pad(values, ((0, 0), (0, extra)))


def stream(block, expert_ids, route, gains, weights):
    gain_dense, gain_expert = gains
    dense_gate, dense_up, dense_down, expert_gate, expert_up, expert_down = weights
    size = lax.axis_size("tensor")
    mine_e, mine_t = lax.axis_index("expert"), lax.axis_index("tensor")
    rows, part = block.shape
    full_width = part * size
    hidden = dense_gate.shape[1]
    local_count, _, hidden_part = expert_gate.shape
    expert_total = local_count * size

    turned = transposed(block)
    arrived = jnp.stack(gathered(turned, "tensor"))
    gain_block = lax.dynamic_slice_in_dim(gain_dense, mine_e * part, part, 0)
    across = mine_e ^ mine_t
    tokens = jnp.concatenate([pick(arrived, d ^ across) for d in range(size)])
    wide = tokens.astype(jnp.float32)
    scaled = (wide * gain_block).astype(jnp.bfloat16)
    squares = two_parts(jnp.sum(wide * wide, axis=1, keepdims=True))
    partial_sums = jnp.concatenate(
        [
            jnp.dot(scaled, dense_gate, preferred_element_type=jnp.float32).astype(jnp.bfloat16),
            jnp.dot(scaled, dense_up, preferred_element_type=jnp.float32).astype(jnp.bfloat16),
            padded_columns(squares),
        ],
        axis=1,
    ).reshape(size, rows, -1)
    sums = traded([partial_sums[d] for d in range(size)], "expert")
    square_sum = sums[:, 2 * hidden : 2 * hidden + 1] + sums[:, 2 * hidden + 1 : 2 * hidden + 2]
    inverse = lax.rsqrt(square_sum / full_width + EPSILON)
    act = jax.nn.silu(sums[:, :hidden] * inverse) * (sums[:, hidden : 2 * hidden] * inverse)

    chosen = expert_ids[:, :, None] == jnp.arange(expert_total, dtype=jnp.int32)
    shares = jnp.sum(jnp.where(chosen, route[:, :, None], 0.0), axis=1)
    carried = jnp.concatenate([act.astype(jnp.bfloat16), padded_columns(two_parts(shares))], axis=1)
    all_carried = jnp.stack(gathered(carried, "expert"))
    down = lax.dot_general(
        all_carried[:, :, :hidden].reshape(size * rows, hidden),
        dense_down,
        (((1,), (1,)), ((), ())),
        preferred_element_type=jnp.float32,
    )
    down = down.astype(jnp.bfloat16).reshape(size, rows, part)
    summed = traded([pick(down, d ^ across) for d in range(size)], "tensor")
    middle_turned = (turned.astype(jnp.float32) + summed).astype(jnp.bfloat16)
    middle = transposed(middle_turned)

    parts = jnp.stack(gathered(middle_turned, "expert"))
    row = jnp.concatenate([pick(parts, b ^ mine_e) for b in range(size)], axis=1)
    normed = normalize(row.astype(jnp.float32), gain_expert).astype(jnp.bfloat16)
    spread = jnp.concatenate(gathered(normed, "tensor"))

    all_shares = jnp.stack(
        [pick(all_carried[:, :, hidden:], d ^ across) for d in range(size)]
    ).reshape(size * rows, -1)
    all_shares = (
        all_shares[:, :expert_total].astype(jnp.float32)
        + all_shares[:, expert_total : 2 * expert_total].astype(jnp.float32)
    )
    own_shares = lax.dynamic_slice_in_dim(all_shares, mine_e * local_count, local_count, 1)
    pieces = []
    for which in range(local_count):
        gate_sums = jnp.dot(spread, expert_gate[which], preferred_element_type=jnp.float32)
        upward = jnp.dot(spread, expert_up[which], preferred_element_type=jnp.float32)
        value = jax.nn.silu(gate_sums) * upward * own_shares[:, which : which + 1]
        pieces.append(value.astype(jnp.bfloat16))
    mixed = jnp.dot(
        jnp.concatenate(pieces, axis=1),
        expert_down.reshape(local_count * hidden_part, full_width),
        preferred_element_type=jnp.float32,
    ).astype(jnp.bfloat16)
    columns = jnp.stack([mixed[:, b * part : (b + 1) * part] for b in range(size)])
    columns = columns.reshape(size, size, rows, part)
    leaving = []
    for d in range(size):
        block_d = pick(columns, mine_t ^ d)
        leaving.append(jnp.concatenate([block_d[j ^ d] for j in range(size)]))
    own_columns = traded(leaving, "tensor").reshape(size, rows, part)
    mixed_here = traded([pick(own_columns, d ^ across) for d in range(size)], "expert")
    final = (middle.astype(jnp.float32) + mixed_here).astype(jnp.bfloat16)
    return middle, final


def square_body(
    activations, expert_ids, route_weights, gain_dense, gain_expert, *weights
):
    segment_index = lax.axis_index("segment")
    block = activations[0]
    ids = pick(expert_ids, segment_index)
    route = pick(route_weights, segment_index)
    middle, final = stream(block, ids, route, (gain_dense, gain_expert), weights)
    other = swap(jnp.where(segment_index == 0, final, middle), "segment", 1)
    own = jnp.where(segment_index == 0, middle, final)
    sections = jnp.where(segment_index == 0, jnp.stack([own, other]), jnp.stack([other, own]))
    return sections[None]


def body(activations, expert_ids, *rest):
    size = lax.axis_size("tensor")
    groups = lax.axis_size("expert")
    segments = lax.axis_size("segment")
    expert_total = rest[4 + 2].shape[0] * groups
    crowded = 2 * expert_ids.shape[2] >= expert_total
    if size == groups and size & (size - 1) == 0 and segments == 2 and crowded:
        return square_body(activations, expert_ids, *rest)
    return general_body(activations, expert_ids, *rest)


def solution(mesh):
    placed = (
        P("segment", "expert", "tensor"),
        P(None, "expert", None),
        P(None, "expert", None),
        P(),
        P(),
        P("expert", "tensor"),
        P("expert", "tensor"),
        P("expert", "tensor"),
        P("expert", None, "tensor"),
        P("expert", None, "tensor"),
        P("expert", "tensor", None),
    )
    return jax.shard_map(
        body,
        mesh=mesh,
        in_specs=placed,
        out_specs=P("segment", None, "expert", "tensor"),
        check_vma=False,
    )
```

```python
import jax
import jax.numpy as jnp
from jax import lax
from jax.experimental import pallas as pl
from jax.experimental.pallas import tpu as pltpu
from jax.sharding import PartitionSpec as P


EPSILON = 1e-06


def shifted(block, axis, distance):
    devices = range(lax.axis_size(axis))
    route = [((i - distance) % len(devices), i) for i in devices]
    return lax.ppermute(block, axis, route)


def normalize(values, gain_row):
    inverse = lax.rsqrt(jnp.mean(values * values, axis=-1, keepdims=True) + EPSILON)
    return values * inverse * gain_row


def dense_prepare(micro_block, gain_dense):
    micro_count, tokens_here, _ = micro_block.shape
    whole_rows = lax.all_gather(micro_block, "tensor", axis=2, tiled=True)
    full_width = whole_rows.shape[2]
    normed = normalize(whole_rows.astype(jnp.float32), gain_dense).astype(jnp.bfloat16)
    return normed.reshape(micro_count * tokens_here, full_width)


def dense_finish(micro_block, partial_value):
    micro_count, tokens_here, _ = micro_block.shape
    summed = lax.psum_scatter(
        partial_value.reshape(micro_count, tokens_here, partial_value.shape[1]).astype(
            jnp.bfloat16
        ),
        "tensor",
        scatter_dimension=2,
        tiled=True,
    ).astype(jnp.float32)
    return (micro_block.astype(jnp.float32) + summed).astype(jnp.bfloat16)


def dense_folded(activations, gain_dense, dense_gate, dense_up, dense_down):
    normed = dense_prepare(activations, gain_dense)
    gate_sums = jnp.dot(
        normed,
        lax.all_gather(dense_gate, "expert", axis=0, tiled=True),
        preferred_element_type=jnp.float32,
    )
    upward = jnp.dot(
        normed,
        lax.all_gather(dense_up, "expert", axis=0, tiled=True),
        preferred_element_type=jnp.float32,
    )
    hidden = (jax.nn.silu(gate_sums) * upward).astype(jnp.bfloat16)
    partial_value = lax.dot_general(
        hidden,
        lax.all_gather(dense_down, "expert", axis=0, tiled=True),
        (((1,), (1,)), ((), ())),
        preferred_element_type=jnp.float32,
    )
    return dense_finish(activations, partial_value)


def route_slots(expert_ids_block, local_count, groups, capacity):
    tokens_here, picks = expert_ids_block.shape
    flat_ids = expert_ids_block.reshape(-1)
    experts_all = local_count * groups
    one_hot = (flat_ids[:, None] == jnp.arange(experts_all, dtype=jnp.int32)[None, :]).astype(
        jnp.int32
    )
    ranks = jnp.sum((jnp.cumsum(one_hot, axis=0) - 1) * one_hot, axis=1)
    slots = (flat_ids % local_count * groups + flat_ids // local_count) * capacity + ranks
    owners = jnp.arange(tokens_here * picks, dtype=jnp.int32) // picks
    sources = jnp.full((experts_all * capacity,), tokens_here, jnp.int32).at[slots].set(owners)
    return (slots, sources)


def place_rows(normed, sources, local_count, groups, capacity):
    padded = jnp.concatenate([normed, jnp.zeros((1, normed.shape[1]), normed.dtype)], axis=0)
    return padded[sources].reshape(local_count, groups, capacity, normed.shape[1])


def expert_block(
    middle, expert_ids_block, route_block, gain_expert, expert_gate, expert_up, expert_down
):
    tokens_here, quarter = middle.shape
    picks = expert_ids_block.shape[1]
    groups = lax.axis_size("expert")
    local_count, full_width, _ = expert_gate.shape
    capacity = min(tokens_here, 2 * (tokens_here * picks // (local_count * groups)))
    slots, sources = route_slots(expert_ids_block, local_count, groups, capacity)
    middle_wide = middle.astype(jnp.float32)
    received_rows = groups * capacity
    tensor_index = lax.axis_index("tensor")
    square_sums = lax.psum(jnp.sum(middle_wide * middle_wide, axis=1), "tensor")
    inverse = lax.rsqrt(square_sums / full_width + EPSILON)
    gain_part = lax.dynamic_slice_in_dim(gain_expert, tensor_index * quarter, quarter, 0)
    normed = (middle_wide * inverse[:, None] * gain_part).astype(jnp.bfloat16)
    outgoing = place_rows(normed, sources, local_count, groups, capacity)
    arrived = lax.all_to_all(outgoing, "expert", split_axis=1, concat_axis=1, tiled=True)
    arrived = arrived.reshape(local_count, received_rows, quarter)
    slice_part = lax.all_gather(arrived, "tensor", axis=2, tiled=True)
    gate_sums = jnp.einsum(
        "lrc,lch->lrh", slice_part, expert_gate, preferred_element_type=jnp.float32
    )
    upward = jnp.einsum("lrc,lch->lrh", slice_part, expert_up, preferred_element_type=jnp.float32)
    hidden = (jax.nn.silu(gate_sums) * upward).astype(jnp.bfloat16)
    partial_value = jnp.einsum(
        "lrh,lhd->lrd", hidden, expert_down, preferred_element_type=jnp.float32
    )
    summed = lax.psum_scatter(
        partial_value.astype(jnp.bfloat16), "tensor", scatter_dimension=2, tiled=True
    )
    returned = lax.all_to_all(
        summed.reshape(local_count, groups, capacity, quarter),
        "expert",
        split_axis=1,
        concat_axis=1,
        tiled=True,
    )
    picked = returned.reshape(local_count * groups * capacity, quarter)[slots]
    picked = picked.reshape(tokens_here, picks, quarter).astype(jnp.float32)
    mixed = jnp.sum(route_block[:, :, None] * picked, axis=1)
    return (middle_wide + mixed).astype(jnp.bfloat16)


def general_body(
    activations,
    expert_ids,
    route_weights,
    gain_dense,
    gain_expert,
    dense_gate,
    dense_up,
    dense_down,
    expert_gate,
    expert_up,
    expert_down,
):
    segment_index = lax.axis_index("segment")
    own_middle = dense_folded(activations, gain_dense, dense_gate, dense_up, dense_down)
    other_middle = shifted(own_middle, "segment", 1)
    middles = jnp.where(
        segment_index == 0,
        jnp.concatenate([own_middle, other_middle], axis=0),
        jnp.concatenate([other_middle, own_middle], axis=0),
    )
    finals = jnp.stack(
        [
            expert_block(
                middles[position],
                expert_ids[position],
                route_weights[position],
                gain_expert,
                expert_gate,
                expert_up,
                expert_down,
            )
            for position in range(middles.shape[0])
        ]
    )
    sections = jnp.where(segment_index == 0, middles, finals)
    return sections[None]


def swap(block, axis, distance):
    devices = range(lax.axis_size(axis))
    return lax.ppermute(block, axis, [(i, i ^ distance) for i in devices])


def transposed(block):
    size = lax.axis_size("tensor")
    route = [(a * size + b, b * size + a) for a in range(size) for b in range(size)]
    return lax.ppermute(block, ("expert", "tensor"), route)


def gathered(block, axis):
    size = lax.axis_size(axis)
    arrived = {d: swap(block, axis, d) for d in range(size - 1, 0, -1)}
    return [block] + [arrived[d] for d in range(1, size)]


def traded(blocks, axis):
    size = lax.axis_size(axis)
    sent = {d: swap(blocks[d].astype(jnp.bfloat16), axis, d) for d in range(size - 1, 0, -1)}
    total = blocks[0].astype(jnp.float32)
    for d in range(1, size):
        total = total + sent[d].astype(jnp.float32)
    return total


def pick(stacked, index):
    return lax.dynamic_index_in_dim(stacked, index, 0, keepdims=False)


LANES = 128
STEPS = 3
ON_CHIP = True
IN_VMEM = pl.BlockSpec(memory_space=pltpu.VMEM)
IN_SMEM = pl.BlockSpec(memory_space=pltpu.SMEM)
IN_PLACE = pl.BlockSpec(memory_space=pltpu.HBM)


def call(kernel, out_shape, operands, specs, limit, flops, moved, scratch=()):
    count = len(out_shape)
    return pl.pallas_call(
        kernel,
        out_shape=out_shape,
        in_specs=specs,
        out_specs=[IN_VMEM] * count,
        scratch_shapes=scratch,
        compiler_params=pltpu.CompilerParams(vmem_limit_bytes=limit),
        cost_estimate=pl.CostEstimate(flops=flops, bytes_accessed=moved, transcendentals=0),
    )(*operands)


def on_chip(array):
    return pltpu.with_memory_space_constraint(array, pltpu.VMEM) if ON_CHIP else array


def fetch_kernel(*refs):
    count = len(refs) // 2
    copies = [
        pltpu.make_async_copy(refs[i], refs[count + i], refs[-1].at[i]) for i in range(count)
    ]
    for copy in copies:
        copy.start()
    for copy in copies:
        copy.wait()


def fetched(arrays):
    return call(
        fetch_kernel,
        [pltpu.VMEM(a.shape, a.dtype) if ON_CHIP else jax.ShapeDtypeStruct(a.shape, a.dtype) for a in arrays],
        arrays,
        [IN_PLACE] * len(arrays),
        1 << 20,
        0,
        sum(a.size * 2 for a in arrays),
        [pltpu.SemaphoreType.DMA((len(arrays),))],
    )


def dense_kernel(across_ref, *refs):
    size = lax.axis_size("tensor")
    blocks, (gain_ref, *weights), outs = refs[:size], refs[size : size + 3], refs[size + 3 :]
    hidden = weights[0].shape[1]
    step = hidden // STEPS
    across = across_ref[0]
    gain = gain_ref[...]
    rows = blocks[0].shape[0]
    scaled = []
    for d in range(size):
        block = blocks[d][...]
        for other in range(1, size):
            block = jnp.where(across == other, blocks[d ^ other][...], block)
        scaled.append((block.astype(jnp.float32) * gain).astype(jnp.bfloat16))
    tokens = jnp.concatenate(scaled)
    for which, weight_ref in enumerate(weights):
        for first in range(0, hidden, step):
            sums = jnp.dot(
                tokens, weight_ref[:, first : first + step], preferred_element_type=jnp.float32
            ).astype(jnp.bfloat16)
            for d in range(size):
                outs[which * size + d][:, first : first + step] = sums[d * rows : (d + 1) * rows]


def expert_kernel(own_ref, *refs):
    size = lax.axis_size("tensor")
    blocks, (share_ref, gate_ref, up_ref, down_ref) = refs[:size], refs[size : size + 4]
    outs = refs[size + 4 :]
    local_count, _, _ = gate_ref.shape
    rows, full_width = blocks[0].shape
    part = full_width // size
    own = own_ref[0]
    spread = jnp.concatenate([block[...] for block in blocks])
    pieces = []
    for which in range(local_count):
        gate = jnp.dot(spread, gate_ref[which], preferred_element_type=jnp.float32)
        up = jnp.dot(spread, up_ref[which], preferred_element_type=jnp.float32)
        value = gate / (1.0 + jnp.exp(-gate)) * up * share_ref[:, which : which + 1]
        pieces.append(value.astype(jnp.bfloat16))
    for d in range(size):
        column = pl.multiple_of((own ^ d) * part, LANES)
        mixed = None
        for which in range(local_count):
            term = jnp.dot(
                pieces[which],
                down_ref[which, :, pl.ds(column, part)],
                preferred_element_type=jnp.float32,
            )
            mixed = term if mixed is None else mixed + term
        mixed = mixed.astype(jnp.bfloat16)
        for j in range(size):
            outs[d][j * rows : (j + 1) * rows] = mixed[(j ^ d) * rows : ((j ^ d) + 1) * rows]


def square_body(activations, expert_ids, route_weights, gain_dense, gain_expert, *weights):
    dense_gate, dense_up, dense_down, expert_gate, expert_up, expert_down = weights
    segment_index = lax.axis_index("segment")
    mine_e, mine_t = lax.axis_index("expert"), lax.axis_index("tensor")
    across = mine_e ^ mine_t
    size = lax.axis_size("tensor")
    block = activations[0]
    rows, part = block.shape
    full_width = part * size
    hidden = dense_gate.shape[1]
    local_count, _, hidden_part = expert_gate.shape
    expert_total = local_count * size
    turned = transposed(block)
    held = fetched([dense_gate, dense_up])
    if ON_CHIP:
        turned, held = lax.optimization_barrier((turned, held))
    arrived = gathered(turned, "tensor")
    gain_block = lax.dynamic_slice_in_dim(gain_dense, mine_e * part, part, 0)
    partial_sums = call(
        dense_kernel,
        [jax.ShapeDtypeStruct((rows, hidden), jnp.bfloat16)] * (2 * size),
        [across[None], *arrived, gain_block[None], *map(on_chip, held)],
        [IN_SMEM] + [IN_VMEM] * (size + 3),
        6 << 20,
        4 * size * rows * part * hidden,
        4 * part * hidden,
    )

    wide = block.astype(jnp.float32)
    squares = sum(gathered(jnp.sum(wide * wide, axis=1), "tensor"))
    inverse = lax.rsqrt(squares / full_width + EPSILON)[:, None]
    ids, route = pick(expert_ids, segment_index), pick(route_weights, segment_index)
    numbers = jnp.arange(expert_total, dtype=jnp.int32)[:, None, None]
    shares = jnp.sum(jnp.where(ids[None] == numbers, route[None], 0.0), axis=2)
    all_shares = jnp.stack(gathered(shares, "expert"))
    own_shares = lax.dynamic_slice_in_dim(all_shares, mine_e * local_count, local_count, 1)
    own_shares = jnp.stack([pick(own_shares, d ^ across) for d in range(size)])
    own_shares = jnp.swapaxes(own_shares, 1, 2)

    gates, ups = partial_sums[:size], partial_sums[size:]
    relayed = swap(ups[3], "expert", 1)
    gate_far = swap(gates[3], "expert", 3)
    gate_next = swap(gates[2], "expert", 2)
    whole = swap(jnp.concatenate([gates[1], ups[1]], axis=1), "expert", 1)
    joined = (ups[2].astype(jnp.float32) + relayed.astype(jnp.float32)).astype(jnp.bfloat16)
    up_next = swap(joined, "expert", 2)
    gate_sums = sum(a.astype(jnp.float32) for a in (gates[0], gate_far, gate_next, whole[:, :hidden]))
    up_sums = sum(a.astype(jnp.float32) for a in (ups[0], up_next, whole[:, hidden:]))
    act = jax.nn.silu(gate_sums * inverse) * (up_sums * inverse)
    act = act.astype(jnp.bfloat16)

    cut = hidden // 2
    act_two = swap(act, "expert", 2)
    act_far = swap(act[:, :cut], "expert", 3)
    act_one = swap(act, "expert", 1)
    act_rest = swap(act_two[:, cut:], "expert", 1)
    act_three = jnp.concatenate([act_far, act_rest], axis=1)
    acts = jnp.concatenate([act, act_one, act_two, act_three])
    down = lax.dot_general(
        acts, dense_down, (((1,), (1,)), ((), ())), preferred_element_type=jnp.float32
    )
    down = down.astype(jnp.bfloat16).reshape(size, rows, part)
    summed = traded([pick(down, d ^ across) for d in range(size)], "tensor")
    middle_turned = (turned.astype(jnp.float32) + summed).astype(jnp.bfloat16)

    parts = jnp.stack(gathered(middle_turned, "expert"))
    row = jnp.concatenate([pick(parts, b ^ mine_e) for b in range(size)], axis=1)
    normed = normalize(row.astype(jnp.float32), gain_expert).astype(jnp.bfloat16)
    experts = [expert_gate, expert_up, expert_down]
    if ON_CHIP:
        normed, experts = lax.optimization_barrier((normed, experts))
    spread = gathered(normed, "tensor")
    experts = fetched(experts)
    columns = call(
        expert_kernel,
        [jax.ShapeDtypeStruct((size * rows, part), jnp.bfloat16)] * size,
        [
            mine_t[None],
            *spread,
            own_shares.reshape(size * rows, local_count),
            *map(on_chip, experts),
        ],
        [IN_SMEM] + [IN_VMEM] * (size + 4),
        12 << 20,
        6 * size * rows * full_width * local_count * hidden_part,
        4 * full_width * size * rows,
    )
    own_columns = traded(columns, "tensor").reshape(size, rows, part)
    mixed = traded([pick(own_columns, d ^ across) for d in range(size)], "expert")
    middle = transposed(middle_turned)
    final = (middle.astype(jnp.float32) + mixed).astype(jnp.bfloat16)
    other = swap(jnp.where(segment_index == 0, final, middle), "segment", 1)
    own = jnp.where(segment_index == 0, middle, final)
    sections = jnp.where(segment_index == 0, jnp.stack([own, other]), jnp.stack([other, own]))
    return sections[None]


def body(activations, expert_ids, *rest):
    size = lax.axis_size("tensor")
    groups = lax.axis_size("expert")
    segments = lax.axis_size("segment")
    expert_total = rest[4 + 2].shape[0] * groups
    crowded = 2 * expert_ids.shape[2] >= expert_total
    if size == groups == 4 and segments == 2 and crowded:
        return square_body(activations, expert_ids, *rest)
    return general_body(activations, expert_ids, *rest)


def solution(mesh):
    placed = (
        P("segment", "expert", "tensor"),
        P(None, "expert", None),
        P(None, "expert", None),
        P(),
        P(),
        P("expert", "tensor"),
        P("expert", "tensor"),
        P("expert", "tensor"),
        P("expert", None, "tensor"),
        P("expert", None, "tensor"),
        P("expert", "tensor", None),
    )
    return jax.shard_map(
        body,
        mesh=mesh,
        in_specs=placed,
        out_specs=P("segment", None, "expert", "tensor"),
        check_vma=False,
    )
```

```python
import jax
import jax.numpy as jnp
from jax import lax
from jax.experimental import pallas as pl
from jax.experimental.pallas import tpu as pltpu
from jax.sharding import PartitionSpec as P


EPSILON = 1e-06


def shifted(block, axis, distance):
    devices = range(lax.axis_size(axis))
    route = [((i - distance) % len(devices), i) for i in devices]
    return lax.ppermute(block, axis, route)


def normalize(values, gain_row):
    inverse = lax.rsqrt(jnp.mean(values * values, axis=-1, keepdims=True) + EPSILON)
    return values * inverse * gain_row


def dense_prepare(micro_block, gain_dense):
    micro_count, tokens_here, _ = micro_block.shape
    whole_rows = lax.all_gather(micro_block, "tensor", axis=2, tiled=True)
    full_width = whole_rows.shape[2]
    normed = normalize(whole_rows.astype(jnp.float32), gain_dense).astype(jnp.bfloat16)
    return normed.reshape(micro_count * tokens_here, full_width)


def dense_finish(micro_block, partial_value):
    micro_count, tokens_here, _ = micro_block.shape
    summed = lax.psum_scatter(
        partial_value.reshape(micro_count, tokens_here, partial_value.shape[1]).astype(
            jnp.bfloat16
        ),
        "tensor",
        scatter_dimension=2,
        tiled=True,
    ).astype(jnp.float32)
    return (micro_block.astype(jnp.float32) + summed).astype(jnp.bfloat16)


def dense_folded(activations, gain_dense, dense_gate, dense_up, dense_down):
    normed = dense_prepare(activations, gain_dense)
    gate_sums = jnp.dot(
        normed,
        lax.all_gather(dense_gate, "expert", axis=0, tiled=True),
        preferred_element_type=jnp.float32,
    )
    upward = jnp.dot(
        normed,
        lax.all_gather(dense_up, "expert", axis=0, tiled=True),
        preferred_element_type=jnp.float32,
    )
    hidden = (jax.nn.silu(gate_sums) * upward).astype(jnp.bfloat16)
    partial_value = lax.dot_general(
        hidden,
        lax.all_gather(dense_down, "expert", axis=0, tiled=True),
        (((1,), (1,)), ((), ())),
        preferred_element_type=jnp.float32,
    )
    return dense_finish(activations, partial_value)


def route_slots(expert_ids_block, local_count, groups, capacity):
    tokens_here, picks = expert_ids_block.shape
    flat_ids = expert_ids_block.reshape(-1)
    experts_all = local_count * groups
    one_hot = (flat_ids[:, None] == jnp.arange(experts_all, dtype=jnp.int32)[None, :]).astype(
        jnp.int32
    )
    ranks = jnp.sum((jnp.cumsum(one_hot, axis=0) - 1) * one_hot, axis=1)
    slots = (flat_ids % local_count * groups + flat_ids // local_count) * capacity + ranks
    owners = jnp.arange(tokens_here * picks, dtype=jnp.int32) // picks
    sources = jnp.full((experts_all * capacity,), tokens_here, jnp.int32).at[slots].set(owners)
    return (slots, sources)


def place_rows(normed, sources, local_count, groups, capacity):
    padded = jnp.concatenate([normed, jnp.zeros((1, normed.shape[1]), normed.dtype)], axis=0)
    return padded[sources].reshape(local_count, groups, capacity, normed.shape[1])


def expert_block(
    middle, expert_ids_block, route_block, gain_expert, expert_gate, expert_up, expert_down
):
    tokens_here, quarter = middle.shape
    picks = expert_ids_block.shape[1]
    groups = lax.axis_size("expert")
    local_count, full_width, _ = expert_gate.shape
    capacity = min(tokens_here, 2 * (tokens_here * picks // (local_count * groups)))
    slots, sources = route_slots(expert_ids_block, local_count, groups, capacity)
    middle_wide = middle.astype(jnp.float32)
    received_rows = groups * capacity
    tensor_index = lax.axis_index("tensor")
    square_sums = lax.psum(jnp.sum(middle_wide * middle_wide, axis=1), "tensor")
    inverse = lax.rsqrt(square_sums / full_width + EPSILON)
    gain_part = lax.dynamic_slice_in_dim(gain_expert, tensor_index * quarter, quarter, 0)
    normed = (middle_wide * inverse[:, None] * gain_part).astype(jnp.bfloat16)
    outgoing = place_rows(normed, sources, local_count, groups, capacity)
    arrived = lax.all_to_all(outgoing, "expert", split_axis=1, concat_axis=1, tiled=True)
    arrived = arrived.reshape(local_count, received_rows, quarter)
    slice_part = lax.all_gather(arrived, "tensor", axis=2, tiled=True)
    gate_sums = jnp.einsum(
        "lrc,lch->lrh", slice_part, expert_gate, preferred_element_type=jnp.float32
    )
    upward = jnp.einsum("lrc,lch->lrh", slice_part, expert_up, preferred_element_type=jnp.float32)
    hidden = (jax.nn.silu(gate_sums) * upward).astype(jnp.bfloat16)
    partial_value = jnp.einsum(
        "lrh,lhd->lrd", hidden, expert_down, preferred_element_type=jnp.float32
    )
    summed = lax.psum_scatter(
        partial_value.astype(jnp.bfloat16), "tensor", scatter_dimension=2, tiled=True
    )
    returned = lax.all_to_all(
        summed.reshape(local_count, groups, capacity, quarter),
        "expert",
        split_axis=1,
        concat_axis=1,
        tiled=True,
    )
    picked = returned.reshape(local_count * groups * capacity, quarter)[slots]
    picked = picked.reshape(tokens_here, picks, quarter).astype(jnp.float32)
    mixed = jnp.sum(route_block[:, :, None] * picked, axis=1)
    return (middle_wide + mixed).astype(jnp.bfloat16)


def general_body(
    activations,
    expert_ids,
    route_weights,
    gain_dense,
    gain_expert,
    dense_gate,
    dense_up,
    dense_down,
    expert_gate,
    expert_up,
    expert_down,
):
    segment_index = lax.axis_index("segment")
    own_middle = dense_folded(activations, gain_dense, dense_gate, dense_up, dense_down)
    other_middle = shifted(own_middle, "segment", 1)
    middles = jnp.where(
        segment_index == 0,
        jnp.concatenate([own_middle, other_middle], axis=0),
        jnp.concatenate([other_middle, own_middle], axis=0),
    )
    finals = jnp.stack(
        [
            expert_block(
                middles[position],
                expert_ids[position],
                route_weights[position],
                gain_expert,
                expert_gate,
                expert_up,
                expert_down,
            )
            for position in range(middles.shape[0])
        ]
    )
    sections = jnp.where(segment_index == 0, middles, finals)
    return sections[None]


def swap(block, axis, distance):
    devices = range(lax.axis_size(axis))
    return lax.ppermute(block, axis, [(i, i ^ distance) for i in devices])


def transposed(block):
    size = lax.axis_size("tensor")
    route = [(a * size + b, b * size + a) for a in range(size) for b in range(size)]
    return lax.ppermute(block, ("expert", "tensor"), route)


def gathered(block, axis):
    size = lax.axis_size(axis)
    arrived = {d: swap(block, axis, d) for d in range(size - 1, 0, -1)}
    return [block] + [arrived[d] for d in range(1, size)]


def traded(blocks, axis):
    size = lax.axis_size(axis)
    sent = {d: swap(blocks[d].astype(jnp.bfloat16), axis, d) for d in range(size - 1, 0, -1)}
    total = blocks[0].astype(jnp.float32)
    for d in range(1, size):
        total = total + sent[d].astype(jnp.float32)
    return total


def pick(stacked, index):
    return lax.dynamic_index_in_dim(stacked, index, 0, keepdims=False)


LANES = 128
STEPS = 3
ON_CHIP = True
IN_VMEM = pl.BlockSpec(memory_space=pltpu.VMEM)
IN_SMEM = pl.BlockSpec(memory_space=pltpu.SMEM)
IN_PLACE = pl.BlockSpec(memory_space=pltpu.HBM)


def call(kernel, out_shape, operands, specs, limit, flops, moved, scratch=()):
    count = len(out_shape)
    return pl.pallas_call(
        kernel,
        out_shape=out_shape,
        in_specs=specs,
        out_specs=[IN_VMEM] * count,
        scratch_shapes=scratch,
        compiler_params=pltpu.CompilerParams(vmem_limit_bytes=limit),
        cost_estimate=pl.CostEstimate(flops=flops, bytes_accessed=moved, transcendentals=0),
    )(*operands)


def on_chip(array):
    return pltpu.with_memory_space_constraint(array, pltpu.VMEM) if ON_CHIP else array


def fetch_kernel(*refs):
    count = len(refs) // 2
    copies = [
        pltpu.make_async_copy(refs[i], refs[count + i], refs[-1].at[i]) for i in range(count)
    ]
    for copy in copies:
        copy.start()
    for copy in copies:
        copy.wait()


def fetched(arrays):
    return call(
        fetch_kernel,
        [pltpu.VMEM(a.shape, a.dtype) if ON_CHIP else jax.ShapeDtypeStruct(a.shape, a.dtype) for a in arrays],
        arrays,
        [IN_PLACE] * len(arrays),
        1 << 20,
        0,
        sum(a.size * 2 for a in arrays),
        [pltpu.SemaphoreType.DMA((len(arrays),))],
    )


def dense_kernel(place_ref, *refs):
    size = lax.axis_size("tensor")
    blocks, (gain_ref, *weights), outs = refs[:size], refs[size : size + 3], refs[size + 3 :]
    hidden = weights[0].shape[1]
    step = hidden // STEPS
    across = place_ref[0]
    rows, part = blocks[0].shape
    gain = gain_ref[:, pl.ds(pl.multiple_of(place_ref[1] * part, LANES), part)]
    scaled = []
    for d in range(size):
        block = blocks[d][...]
        for other in range(1, size):
            block = jnp.where(across == other, blocks[d ^ other][...], block)
        scaled.append((block.astype(jnp.float32) * gain).astype(jnp.bfloat16))
    tokens = jnp.concatenate(scaled)
    for which, weight_ref in enumerate(weights):
        for first in range(0, hidden, step):
            sums = jnp.dot(
                tokens, weight_ref[:, first : first + step], preferred_element_type=jnp.float32
            ).astype(jnp.bfloat16)
            for d in range(size):
                outs[which * size + d][:, first : first + step] = sums[d * rows : (d + 1) * rows]


def expert_kernel(own_ref, *refs):
    size = lax.axis_size("tensor")
    blocks, (share_ref, gate_ref, up_ref, down_ref) = refs[:size], refs[size : size + 4]
    outs = refs[size + 4 :]
    local_count, _, _ = gate_ref.shape
    rows, full_width = blocks[0].shape
    part = full_width // size
    own = own_ref[0]
    spread = jnp.concatenate([block[...] for block in blocks])
    pieces = []
    for which in range(local_count):
        gate = jnp.dot(spread, gate_ref[which], preferred_element_type=jnp.float32)
        up = jnp.dot(spread, up_ref[which], preferred_element_type=jnp.float32)
        value = gate / (1.0 + jnp.exp(-gate)) * up * share_ref[:, which : which + 1]
        pieces.append(value.astype(jnp.bfloat16))
    for d in range(size):
        column = pl.multiple_of((own ^ d) * part, LANES)
        mixed = None
        for which in range(local_count):
            term = jnp.dot(
                pieces[which],
                down_ref[which, :, pl.ds(column, part)],
                preferred_element_type=jnp.float32,
            )
            mixed = term if mixed is None else mixed + term
        mixed = mixed.astype(jnp.bfloat16)
        for j in range(size):
            outs[d][j * rows : (j + 1) * rows] = mixed[(j ^ d) * rows : ((j ^ d) + 1) * rows]


def square_body(activations, expert_ids, route_weights, gain_dense, gain_expert, *weights):
    dense_gate, dense_up, dense_down, expert_gate, expert_up, expert_down = weights
    segment_index = lax.axis_index("segment")
    mine_e, mine_t = lax.axis_index("expert"), lax.axis_index("tensor")
    across = mine_e ^ mine_t
    size = lax.axis_size("tensor")
    block = activations[0]
    rows, part = block.shape
    full_width = part * size
    hidden = dense_gate.shape[1]
    local_count, _, hidden_part = expert_gate.shape
    expert_total = local_count * size
    turned = transposed(block)
    held = fetched([dense_gate, dense_up])
    if ON_CHIP:
        turned, held = lax.optimization_barrier((turned, held))
    arrived = gathered(turned, "tensor")
    partial_sums = call(
        dense_kernel,
        [jax.ShapeDtypeStruct((rows, hidden), jnp.bfloat16)] * (2 * size),
        [jnp.stack([across, mine_e]), *arrived, gain_dense[None], *map(on_chip, held)],
        [IN_SMEM] + [IN_VMEM] * (size + 3),
        6 << 20,
        4 * size * rows * part * hidden,
        4 * part * hidden,
    )

    if ON_CHIP:
        first, expert_ids, route_weights = lax.optimization_barrier(
            (partial_sums[0], expert_ids, route_weights)
        )
        partial_sums = [first, *partial_sums[1:]]

    wide = block.astype(jnp.float32)
    squares = sum(gathered(jnp.sum(wide * wide, axis=1), "tensor"))
    inverse = lax.rsqrt(squares / full_width + EPSILON)[:, None]
    ids, route = pick(expert_ids, segment_index), pick(route_weights, segment_index)
    numbers = jnp.arange(expert_total, dtype=jnp.int32)[:, None, None]
    shares = jnp.sum(jnp.where(ids[None] == numbers, route[None], 0.0), axis=2)
    all_shares = jnp.stack(gathered(shares, "expert"))
    own_shares = lax.dynamic_slice_in_dim(all_shares, mine_e * local_count, local_count, 1)
    own_shares = jnp.stack([pick(own_shares, d ^ across) for d in range(size)])
    own_shares = jnp.swapaxes(own_shares, 1, 2)

    gates, ups = partial_sums[:size], partial_sums[size:]
    relayed = swap(ups[3], "expert", 1)
    gate_far = swap(gates[3], "expert", 3)
    gate_next = swap(gates[2], "expert", 2)
    whole = swap(jnp.concatenate([gates[1], ups[1]], axis=1), "expert", 1)
    joined = (ups[2].astype(jnp.float32) + relayed.astype(jnp.float32)).astype(jnp.bfloat16)
    up_next = swap(joined, "expert", 2)
    gate_sums = sum(a.astype(jnp.float32) for a in (gates[0], gate_far, gate_next, whole[:, :hidden]))
    up_sums = sum(a.astype(jnp.float32) for a in (ups[0], up_next, whole[:, hidden:]))
    act = jax.nn.silu(gate_sums * inverse) * (up_sums * inverse)
    act = act.astype(jnp.bfloat16)

    act_two = swap(act, "expert", 2)
    act_one = swap(act, "expert", 1)
    act_three = swap(act_two, "expert", 1)
    acts = jnp.concatenate([act, act_one, act_two, act_three])
    down = lax.dot_general(
        acts, dense_down, (((1,), (1,)), ((), ())), preferred_element_type=jnp.float32
    )
    down = down.astype(jnp.bfloat16).reshape(size, rows, part)
    summed = traded([pick(down, d ^ across) for d in range(size)], "tensor")
    middle_turned = (turned.astype(jnp.float32) + summed).astype(jnp.bfloat16)

    parts = jnp.stack(gathered(middle_turned, "expert"))
    row = jnp.concatenate([pick(parts, b ^ mine_e) for b in range(size)], axis=1)
    normed = normalize(row.astype(jnp.float32), gain_expert).astype(jnp.bfloat16)
    experts = [expert_gate, expert_up, expert_down]
    if ON_CHIP:
        normed, experts = lax.optimization_barrier((normed, experts))
    spread = gathered(normed, "tensor")
    experts = fetched(experts)
    columns = call(
        expert_kernel,
        [jax.ShapeDtypeStruct((size * rows, part), jnp.bfloat16)] * size,
        [
            mine_t[None],
            *spread,
            own_shares.reshape(size * rows, local_count),
            *map(on_chip, experts),
        ],
        [IN_SMEM] + [IN_VMEM] * (size + 4),
        12 << 20,
        6 * size * rows * full_width * local_count * hidden_part,
        4 * full_width * size * rows,
    )
    own_columns = traded(columns, "tensor").reshape(size, rows, part)
    mixed = traded([pick(own_columns, d ^ across) for d in range(size)], "expert")
    middle = transposed(middle_turned)
    final = (middle.astype(jnp.float32) + mixed).astype(jnp.bfloat16)
    other = swap(jnp.where(segment_index == 0, final, middle), "segment", 1)
    own = jnp.where(segment_index == 0, middle, final)
    sections = jnp.where(segment_index == 0, jnp.stack([own, other]), jnp.stack([other, own]))
    return sections[None]


def body(activations, expert_ids, *rest):
    size = lax.axis_size("tensor")
    groups = lax.axis_size("expert")
    segments = lax.axis_size("segment")
    expert_total = rest[4 + 2].shape[0] * groups
    crowded = 2 * expert_ids.shape[2] >= expert_total
    if size == groups == 4 and segments == 2 and crowded:
        return square_body(activations, expert_ids, *rest)
    return general_body(activations, expert_ids, *rest)


def solution(mesh):
    placed = (
        P("segment", "expert", "tensor"),
        P(None, "expert", None),
        P(None, "expert", None),
        P(),
        P(),
        P("expert", "tensor"),
        P("expert", "tensor"),
        P("expert", "tensor"),
        P("expert", None, "tensor"),
        P("expert", None, "tensor"),
        P("expert", "tensor", None),
    )
    return jax.shard_map(
        body,
        mesh=mesh,
        in_specs=placed,
        out_specs=P("segment", None, "expert", "tensor"),
        check_vma=False,
    )
```
